32 devices in a mesh: people: 8 (over z, x), var: 4 (over y, core).
Axes of the slice: x: 2, y: 2, z: 4, core: 2. Of those that a mesh axis runs over, the one named last changes fastest.
Arguments:
- genotypes: bfloat16 [4096, 2048], P('people', 'var'), may hold values from -6 to 6
- kin_diag: bfloat16 [16, 256, 256], P('people'), may hold values from -0.375 to 0.375
- kin_blocks: bfloat16 [256, 256, 256], P('people'), may hold values from -0.375 to 0.375
- kin_pairs: int32 [256, 2], replicated, may hold values from 0 to 15, as said below
- pair_count: int32 [8], replicated, may hold values from 24 to 32, as said below
- gene_counts: int32 [64], replicated, may hold values from 1 to 1024, 2048 in all
Outputs:
- gene_variance: float32 [2048, 2048], P(('var', 'people'))
The draws below stay inside these ranges and needn't reach their ends.
Inputs may be any that keep to these rules, and one draw needn't show every extreme that they name: `kin_pairs`: slots 32 d to 32 d + 31 belong to index d of people: their row block is one of d's blocks d * 2 to d * 2 + 1, their column block is held by another index of people, and among d's live slots at most 5 slots name column blocks held by any one index; some index of people reaches 5 with one index. `pair_count`: some index of people has all 32 slots live.
All inputs are finite; a program needn't handle non-finite values.
Results may differ from the reference program's by a relative error of at most 0.0029.
Values may be sent and summed in bfloat16 or wider, within the bound.
A program may use at most 128 MiB of HBM per device.

```python
import math
import jax
import jax.numpy as jnp
import numpy as np
from jax import lax

BLOCK = 256
BLK_DEV = 2
PAIR_DEV = 32
GENES = 64
BLOCKS = 16
PERSONS = 4096
PAIRS = 256
VARIANTS = 2048
GENE_MOST = 1024


def draw_kin_pairs(key, part):
    owners = PAIRS // PAIR_DEV
    first_key, second_key, third_key = jax.random.split(jax.random.fold_in(key, 11), 3)
    owner_keys = jax.random.split(first_key, owners)
    scores = jax.vmap(lambda one_key: jax.random.permutation(one_key, owners - 1))(owner_keys).astype(jnp.int32)
    scores = scores.at[:, owners - 2].set(-1)
    scores = scores.at[:, owners // 2 - 1].set(-2)
    sequence = 1 + jnp.argsort(scores, axis=1, stable=True).astype(jnp.int32)
    positions = jnp.arange(PAIR_DEV, dtype=jnp.int32) % (owners - 1)
    offsets = jnp.take(sequence, positions, axis=1)
    home = jnp.arange(owners, dtype=jnp.int32)[:, None]
    target = (home + offsets) % owners
    row_block = home * BLK_DEV + jax.random.randint(second_key, (owners, PAIR_DEV), 0, BLK_DEV)
    col_block = target * BLK_DEV + jax.random.randint(third_key, (owners, PAIR_DEV), 0, BLK_DEV)
    return jnp.stack([row_block, col_block], axis=-1).reshape(PAIRS, 2).astype(jnp.int32)


def draw_pair_count(key, part):
    owners = PAIRS // PAIR_DEV
    first_key, second_key = jax.random.split(jax.random.fold_in(key, 23), 2)
    counts = jax.random.randint(first_key, (owners,), PAIR_DEV - PAIR_DEV // 4, PAIR_DEV + 1)
    fullest = jax.random.randint(second_key, (), 0, owners)
    return counts.at[fullest].set(PAIR_DEV).astype(jnp.int32)


def level_of(rng, extent, shards, least, top_value):
    def one(dim, shards_of):
        draws = jax.random.uniform(jax.random.fold_in(jax.random.fold_in(rng, 6), dim), (shards_of,), jnp.float32, least / len(shards), top_value / len(shards))
        return jnp.repeat(jnp.exp(draws), extent[dim] // shards_of).reshape((-1,) + (1,) * (len(extent) - dim - 1))

    loudness = one(*shards[0])
    for cut in shards[1:]:
        loudness = loudness * one(*cut)
    return loudness


def split_up(amount, total, bound, skew):
    portions = [(1 << 20) // math.isqrt(rank ** skew) + 1 for rank in range(2, amount + 1)]
    rest, given = total - bound - (amount - 1), [1] * (amount - 1)
    while rest > 0:
        candidates = [i for i in range(amount - 1) if given[i] < bound]
        pool, left = sum([portions[i] for i in candidates]), rest
        for i in candidates:
            extra = min(bound - given[i], max(1, left * portions[i] // pool), rest)
            given[i] = given[i] + extra
            rest = rest - extra
    return np.array([bound] + given)


def uneven(own_key, number_of, total, most, skew):
    if number_of == 2:
        one = jax.random.randint(own_key, (), max(1, total - most), min(most, total - 1) + 1)
        return jnp.stack([one, total - one])
    tallies = jnp.asarray(split_up(number_of, total, most, skew), jnp.int32)
    twos = (number_of - 1) // 2
    source_of, taker = tallies[1:1 + 2 * twos:2], tallies[2:2 + 2 * twos:2]
    room = jnp.minimum(source_of - 1, most - taker)
    passed = jax.random.randint(jax.random.fold_in(own_key, 1), (twos,), 0, 1 << 20) % (room + 1)
    tallies = tallies.at[1:1 + 2 * twos:2].set(source_of - passed).at[2:2 + 2 * twos:2].set(taker + passed)
    return tallies[jax.random.permutation(jax.random.fold_in(own_key, 2), number_of)]


def centred(stream_key, extent, spread, limit, shards=(), kind=jnp.bfloat16):
    entries = jax.random.normal(stream_key, extent, jnp.float32) * spread
    if len(shards) > 0:
        entries = level_of(stream_key, extent, shards, -0.22, 0.18) * entries
    return jnp.clip(entries, min=-limit, max=limit).astype(kind)


def setup_inputs(seed: int = 0) -> dict:
    seeds = jax.random.split(jax.random.key(seed), 7)
    genotypes = centred(seeds[0], (PERSONS, VARIANTS), 1.0, 6.0, ((0, 8), (1, 4)))
    kin_diag = centred(seeds[1], (BLOCKS, BLOCK, BLOCK), BLOCK ** -0.5, 0.375, ((0, 8),))
    kin_blocks = centred(seeds[2], (PAIRS, BLOCK, BLOCK), BLOCK ** -0.5, 0.375, ((0, 8),))
    kin_pairs = draw_kin_pairs(jax.random.fold_in(seeds[6], 71), 0)
    pair_count = draw_pair_count(jax.random.fold_in(seeds[6], 71), 0)
    gene_counts = uneven(seeds[5], GENES, VARIANTS, GENE_MOST, 2).astype(jnp.int32)
    return dict(genotypes=genotypes, kin_diag=kin_diag, kin_blocks=kin_blocks, kin_pairs=kin_pairs, pair_count=pair_count, gene_counts=gene_counts)


def gene_index(positions, gene_counts):
    gene_ends = jnp.cumsum(gene_counts)
    return lax.optimization_barrier(jnp.sum((positions[:, None] >= gene_ends[None, :]).astype(jnp.int32), axis=1))

def reference(genotypes, kin_diag, kin_blocks, kin_pairs, pair_count, gene_counts):
    geno_float = genotypes.astype(jnp.float32)
    geno_blocks = geno_float.reshape(BLOCKS, BLOCK, VARIANTS)
    kin_times = jnp.einsum('bij,bjv->biv', kin_diag.astype(jnp.float32), geno_blocks, precision=lax.Precision.HIGHEST)

    def add_pair(slot, carry):
        row_block = kin_pairs[slot, 0]
        col_block = kin_pairs[slot, 1]
        is_live = (slot % PAIR_DEV < pair_count[slot // PAIR_DEV]).astype(jnp.float32)
        source = lax.dynamic_index_in_dim(geno_blocks, col_block, 0, keepdims=False)
        weights = lax.dynamic_index_in_dim(kin_blocks, slot, 0, keepdims=False).astype(jnp.float32)
        product = jnp.dot(weights, source, precision=lax.Precision.HIGHEST) * is_live
        return carry.at[row_block].add(product)
    kin_times = lax.fori_loop(0, PAIRS, add_pair, kin_times)
    kin_rounded = kin_times.reshape(PERSONS, VARIANTS).astype(jnp.bfloat16)
    cross = jnp.dot(geno_float.T, kin_rounded.astype(jnp.float32), precision=lax.Precision.HIGHEST)
    scaling = 1.0 / math.sqrt(PERSONS)
    gene_ids = gene_index(jnp.arange(VARIANTS, dtype=jnp.int32), gene_counts)
    same_gene = gene_ids[:, None] == gene_ids[None, :]
    return jnp.where(same_gene, (cross + cross.T) * (0.5 * scaling), jnp.float32(0.0))
```

```python
import functools
import math

import jax
import jax.numpy as jnp
from jax import lax
from jax.experimental import pallas as pl
from jax.experimental.pallas import tpu as pltpu
from jax.sharding import PartitionSpec as P

BLOCK = 256
SUB = 2
CORES = 2
MESH = pl.DeviceIdType.MESH


def ring_place(index, nz, nx):
    z, x = index // nx, index % nx
    back = nz - 1 - z
    along = jnp.where(back % 2 == 0, x - 1, nx - 1 - x)
    return jnp.where(x == 0, z, nz + back * (nx - 1) + along)


def ring_index(place, nz, nx):
    rest = jnp.where(place < nz, 0, place - nz)
    back, along = rest // (nx - 1), rest % (nx - 1)
    x = jnp.where(back % 2 == 0, 1 + along, nx - 1 - along)
    return jnp.where(place < nz, place * nx, (nz - 1 - back) * nx + x)


def kernel(people, var, g_ref, kd_hbm, kb_hbm, pairs_hbm, cnt_ref, gc_ref, out_ref,
           gall, gvar, krv, kd, kb, acc, g_t, kr_t, pbuf, rbuf, rid, cid, pairs_s,
           ring_send, ring_recv, var_send, var_recv, sum_send, sum_recv, load_sem):
    rows, cols = g_ref.shape
    nx = math.isqrt(people // 2)
    nz = people // nx
    ny = var // CORES
    slots = kb.shape[0]
    me, q = lax.axis_index("people"), lax.axis_index("var")
    y, core = q // CORES, q % CORES
    other = y * CORES + (CORES - 1 - core)

    loads = [
        pltpu.make_async_copy(pairs_hbm.at[pl.ds(me * slots, slots)], pairs_s, load_sem.at[0]),
        pltpu.make_async_copy(kd_hbm, kd, load_sem.at[1]),
        pltpu.make_async_copy(kb_hbm, kb, load_sem.at[2]),
    ]
    for load in loads:
        load.start()

    barrier = pltpu.get_barrier_semaphore()
    for step in range(1, people):
        pl.semaphore_signal(barrier, inc=1, device_id=(lax.rem(me + step, people), q), device_id_type=MESH)
    for step in range(1, var):
        pl.semaphore_signal(barrier, inc=1, device_id=(me, lax.rem(q + step, var)), device_id_type=MESH)
    pl.semaphore_wait(barrier, people + var - 2)

    place = ring_place(me, nz, nx)
    right = ring_index(lax.rem(place + 1, people), nz, nx)
    left = ring_index(lax.rem(place + people - 1, people), nz, nx)
    part = BLOCK // SUB

    def ring_copy(step, way, sub):
        shift = people - step if way == 0 else step
        source = ring_index(lax.rem(place + shift, people), nz, nx)
        view = gall.at[2 * source + way, pl.ds(sub * part, part)]
        return pltpu.make_async_remote_copy(
            src_ref=view, dst_ref=view,
            send_sem=ring_send.at[step, way, sub], recv_sem=ring_recv.at[step, way, sub],
            device_id=(right if way == 0 else left, q), device_id_type=MESH)

    def var_copy(buf, use, slot, target, sem):
        return pltpu.make_async_remote_copy(
            src_ref=buf.at[slot], dst_ref=buf.at[slot],
            send_sem=var_send.at[use, sem], recv_sem=var_recv.at[use, sem],
            device_id=(me, target), device_id_type=MESH)

    def var_first(buf, use):
        for dy in range(1, ny):
            var_copy(buf, use, q, lax.rem(y + dy, ny) * CORES + core, dy - 1).start()
        var_copy(buf, use, q, other, ny - 1).start()

    def var_forward(buf, use):
        for dy in range(1, ny):
            slot = lax.rem(y + ny - dy, ny) * CORES + core
            var_copy(buf, use, slot, other, dy - 1).wait_recv()
            var_copy(buf, use, slot, other, ny - 1 + dy).start()

    def var_finish(buf, use):
        for sem in range(ny - 1, 2 * ny - 1):
            var_copy(buf, use, q, other, sem).wait_recv()
        for sem in range(2 * ny - 1):
            var_copy(buf, use, q, other, sem).wait_send()

    for half in range(rows // BLOCK):
        gall[2 * me + half] = g_ref[pl.ds(half * BLOCK, BLOCK), :]
    gvar[q] = g_ref[...]
    for sub in range(SUB):
        for way in range(2):
            ring_copy(0, way, sub).start()
    var_first(gvar, 0)

    g_t[...] = g_ref[...].T
    rid[...] = jnp.zeros_like(rid)
    cid[...] = jnp.zeros_like(cid)

    def gene_step(gene, end):
        end = end + gc_ref[gene]
        row_ids = q * cols + lax.broadcasted_iota(jnp.int32, rid.shape, 0)
        col_ids = lax.broadcasted_iota(jnp.int32, cid.shape, 1)
        rid[...] += (row_ids >= end).astype(jnp.int32)
        cid[...] += (col_ids >= end).astype(jnp.int32)
        return end

    lax.fori_loop(0, gc_ref.shape[0], gene_step, jnp.int32(0))

    def ring_step(step, carry):
        for sub in range(SUB):
            for way in range(2):
                ring_copy(step - 1, way, sub).wait_recv()
                ring_copy(step, way, sub).start()
        return carry

    lax.fori_loop(1, people - 1, ring_step, 0)
    var_forward(gvar, 0)
    for load in loads:
        load.wait()
    for half in range(rows // BLOCK):
        acc[half] = jnp.dot(kd[half], g_ref[pl.ds(half * BLOCK, BLOCK), :], preferred_element_type=jnp.float32)
    for sub in range(SUB):
        for way in range(2):
            ring_copy(people - 2, way, sub).wait_recv()

    def pair_step(slot, carry):
        row = pairs_s[slot, 0] - me * 2
        col = pairs_s[slot, 1]
        live = slot < cnt_ref[me]
        term = jnp.dot(kb[slot], gall[col], preferred_element_type=jnp.float32)
        for half in range(2):
            weight = jnp.where(live & (row == half), 1.0, 0.0).astype(jnp.float32)
            acc[half] += term * weight
        return carry

    lax.fori_loop(0, slots, pair_step, 0)
    for half in range(2):
        krv[q, pl.ds(half * BLOCK, BLOCK), :] = acc[half].astype(jnp.bfloat16)
    var_first(krv, 1)
    kr_t[...] = krv[q].T

    def ring_drain(step, carry):
        for sub in range(SUB):
            for way in range(2):
                ring_copy(step, way, sub).wait_send()
        return carry

    lax.fori_loop(0, people - 1, ring_drain, 0)
    var_finish(gvar, 0)
    var_forward(krv, 1)
    var_finish(krv, 1)

    width = pbuf.shape[2]
    chunk = rows // people
    tile = BLOCK
    per_tile = tile // chunk

    def sum_copy(target):
        return pltpu.make_async_remote_copy(
            src_ref=pbuf.at[target], dst_ref=rbuf.at[me],
            send_sem=sum_send.at[target], recv_sem=sum_recv.at[me],
            device_id=(target, q), device_id_type=MESH)

    for t in range(cols // tile):
        span = pl.ds(t * tile, tile)
        row_gene = rid[span, 0:1]
        for j in range(var // 2):
            total = jnp.zeros((tile, cols), jnp.float32)
            for k in (j, j + var // 2):
                value = jnp.dot(g_t[span, :], krv[k], preferred_element_type=jnp.float32)
                value += jnp.dot(kr_t[span, :], gvar[k], preferred_element_type=jnp.float32)
                same = row_gene == cid[0:1, k * cols:(k + 1) * cols]
                total = jnp.where(same, value, total)
            pbuf[t * per_tile:(t + 1) * per_tile, :, j * cols:(j + 1) * cols] = (
                total.astype(jnp.bfloat16).reshape(per_tile, chunk, cols))
        for k in range(per_tile):
            target = t * per_tile + k

            @pl.when(target != me)
            def _():
                sum_copy(target).start()

    own = rid[pl.ds(me * chunk, chunk), 0:1]
    final = pbuf[me].astype(jnp.float32)
    for step in range(1, people):
        source = lax.rem(me + step, people)
        pltpu.make_async_remote_copy(
            src_ref=pbuf.at[source], dst_ref=rbuf.at[source],
            send_sem=sum_send.at[source], recv_sem=sum_recv.at[source],
            device_id=(source, q), device_id_type=MESH).wait_recv()
        final += rbuf[source].astype(jnp.float32)
    final = final * (0.5 / math.sqrt(rows * people))
    for k in range(2):
        same = own == cid[0:1, k * width:(k + 1) * width]
        out_ref[:, k * width:(k + 1) * width] = jnp.where(same, final, 0.0)
    for step in range(1, people):
        sum_copy(lax.rem(me + step, people)).wait_send()


def body(people, var, genotypes, kin_diag, kin_blocks, kin_pairs, pair_count, gene_counts):
    rows, cols = genotypes.shape
    slots = kin_blocks.shape[0]
    total = cols * var
    chunk = rows // people
    ny = var // CORES
    bf16, f32 = jnp.bfloat16, jnp.float32
    anywhere = pl.BlockSpec(memory_space=pl.ANY)
    vmem = pl.BlockSpec(memory_space=pltpu.VMEM)
    smem = pl.BlockSpec(memory_space=pltpu.SMEM)
    dma = pltpu.SemaphoreType.DMA
    return pl.pallas_call(
        functools.partial(kernel, people, var),
        out_shape=jax.ShapeDtypeStruct((chunk, total), f32),
        in_specs=[vmem, anywhere, anywhere, anywhere, smem, smem],
        out_specs=vmem,
        scratch_shapes=[
            pltpu.VMEM((2 * people, BLOCK, cols), bf16),
            pltpu.VMEM((var, rows, cols), bf16),
            pltpu.VMEM((var, rows, cols), bf16),
            pltpu.VMEM(kin_diag.shape, bf16),
            pltpu.VMEM(kin_blocks.shape, bf16),
            pltpu.VMEM((2, BLOCK, cols), f32),
            pltpu.VMEM((cols, rows), bf16),
            pltpu.VMEM((cols, rows), bf16),
            pltpu.VMEM((people, chunk, total // 2), bf16),
            pltpu.VMEM((people, chunk, total // 2), bf16),
            pltpu.VMEM((cols, 128), jnp.int32),
            pltpu.VMEM((8, total), jnp.int32),
            pltpu.SMEM((slots, 2), jnp.int32),
            dma((people - 1, 2, SUB)),
            dma((people - 1, 2, SUB)),
            dma((2, 2 * ny - 1)),
            dma((2, 2 * ny - 1)),
            dma((people,)),
            dma((people,)),
            dma((3,)),
        ],
        compiler_params=pltpu.CompilerParams(
            collective_id=0, has_side_effects=True, vmem_limit_bytes=56 << 20),
    )(genotypes, kin_diag, kin_blocks, kin_pairs, pair_count, gene_counts)


def solution(mesh):
    placed = (P("people", "var"), P("people", None, None), P("people", None, None), P(), P(), P())
    return jax.shard_map(
        functools.partial(body, mesh.shape["people"], mesh.shape["var"]),
        mesh=mesh, in_specs=placed, out_specs=P(("var", "people"), None), check_vma=False,
    )
```

```python
import functools
import math

import jax
import jax.numpy as jnp
from jax import lax
from jax.experimental import pallas as pl
from jax.experimental.pallas import tpu as pltpu
from jax.sharding import PartitionSpec as P

BLOCK = 256
SUB = 2
CORES = 2
MESH = pl.DeviceIdType.MESH


def ring_place(index, nz, nx):
    z, x = index // nx, index % nx
    back = nz - 1 - z
    along = jnp.where(back % 2 == 0, x - 1, nx - 1 - x)
    return jnp.where(x == 0, z, nz + back * (nx - 1) + along)


def ring_index(place, nz, nx):
    rest = jnp.where(place < nz, 0, place - nz)
    back, along = rest // (nx - 1), rest % (nx - 1)
    x = jnp.where(back % 2 == 0, 1 + along, nx - 1 - along)
    return jnp.where(place < nz, place * nx, (nz - 1 - back) * nx + x)


def kernel(people, var, g_ref, kd_hbm, kb_hbm, pairs_ref, cnt_ref, gc_ref, out_ref,
           gall_a, gall_b, gvar, krv_a, krv_b, kd, kb, acc, g_t, kr_t, pbuf, rbuf, rid, cid,
           ring_send, ring_recv, var_send, var_recv, sum_send, sum_recv, load_sem):
    rows, cols = g_ref.shape
    wide = cols // 2
    nx = math.isqrt(people // 2)
    nz = people // nx
    ny = var // CORES
    slots = kb.shape[0]
    galls, krvs = (gall_a, gall_b), (krv_a, krv_b)
    me, q = lax.axis_index("people"), lax.axis_index("var")
    y, core = q // CORES, q % CORES
    other = y * CORES + (CORES - 1 - core)

    loads = [
        pltpu.make_async_copy(kd_hbm, kd, load_sem.at[0]),
        pltpu.make_async_copy(kb_hbm, kb, load_sem.at[1]),
    ]
    for load in loads:
        load.start()

    barrier = pltpu.get_barrier_semaphore()
    for step in range(1, people):
        pl.semaphore_signal(barrier, inc=1, device_id=(lax.rem(me + step, people), q), device_id_type=MESH)
    for step in range(1, var):
        pl.semaphore_signal(barrier, inc=1, device_id=(me, lax.rem(q + step, var)), device_id_type=MESH)

    for h in range(2):
        for half in range(2):
            galls[h][2 * me + half] = g_ref[pl.ds(half * BLOCK, BLOCK), h * wide:(h + 1) * wide]
    gvar[q] = g_ref[...]
    pl.semaphore_wait(barrier, people + var - 2)

    place = ring_place(me, nz, nx)
    right = ring_index(lax.rem(place + 1, people), nz, nx)
    left = ring_index(lax.rem(place + people - 1, people), nz, nx)
    part = BLOCK // SUB

    def ring_copy(h, step, way, sub):
        shift = people - step if way == 0 else step
        source = ring_index(lax.rem(place + shift, people), nz, nx)
        view = galls[h].at[2 * source + way, pl.ds(sub * part, part)]
        return pltpu.make_async_remote_copy(
            src_ref=view, dst_ref=view,
            send_sem=ring_send.at[h, step, way, sub], recv_sem=ring_recv.at[h, step, way, sub],
            device_id=(right if way == 0 else left, q), device_id_type=MESH)

    def ring_start(h):
        for sub in range(SUB):
            for way in range(2):
                ring_copy(h, 0, way, sub).start()

    def ring_step(h, step):
        for sub in range(SUB):
            for way in range(2):
                ring_copy(h, step - 1, way, sub).wait_recv()
                ring_copy(h, step, way, sub).start()

    def ring_last(h):
        for sub in range(SUB):
            for way in range(2):
                ring_copy(h, people - 2, way, sub).wait_recv()

    def var_copy(buf, use, slot, target, sem):
        return pltpu.make_async_remote_copy(
            src_ref=buf.at[slot], dst_ref=buf.at[slot],
            send_sem=var_send.at[use, sem], recv_sem=var_recv.at[use, sem],
            device_id=(me, target), device_id_type=MESH)

    def var_first(buf, use):
        for dy in range(1, ny):
            var_copy(buf, use, q, lax.rem(y + dy, ny) * CORES + core, dy - 1).start()
        var_copy(buf, use, q, other, ny - 1).start()

    def var_forward(buf, use):
        for dy in range(1, ny):
            slot = lax.rem(y + ny - dy, ny) * CORES + core
            var_copy(buf, use, slot, other, dy - 1).wait_recv()
            var_copy(buf, use, slot, other, ny - 1 + dy).start()

    def var_finish(buf, use):
        for sem in range(ny - 1, 2 * ny - 1):
            var_copy(buf, use, q, other, sem).wait_recv()
        for sem in range(2 * ny - 1):
            var_copy(buf, use, q, other, sem).wait_send()

    def gene_step(gene, end):
        end = end + gc_ref[gene]
        row_ids = q * cols + lax.broadcasted_iota(jnp.int32, rid.shape, 0)
        col_ids = lax.broadcasted_iota(jnp.int32, cid.shape, 1)
        rid[...] += (row_ids >= end).astype(jnp.int32)
        cid[...] += (col_ids >= end).astype(jnp.int32)
        return end

    def diag_terms(h):
        for half in range(2):
            acc[half] = jnp.dot(
                kd[half], g_ref[pl.ds(half * BLOCK, BLOCK), h * wide:(h + 1) * wide],
                preferred_element_type=jnp.float32)

    def pair_terms(h, first, last):
        def pair_step(slot, carry):
            row = pairs_ref[0, me * slots + slot] - me * 2
            col = pairs_ref[1, me * slots + slot]
            live = slot < cnt_ref[me]
            term = jnp.dot(kb[slot], galls[h][col], preferred_element_type=jnp.float32)
            for half in range(2):
                weight = jnp.where(live & (row == half), 1.0, 0.0).astype(jnp.float32)
                acc[half] += term * weight
            return carry

        lax.fori_loop(first, last, pair_step, 0)

    def kin_out(h):
        for half in range(2):
            krvs[h][q, pl.ds(half * BLOCK, BLOCK), :] = acc[half].astype(jnp.bfloat16)
        var_first(krvs[h], 1 + h)
        kr_t[h * wide:(h + 1) * wide, :] = krvs[h][q].T

    ring_start(0)
    var_first(gvar, 0)
    rid[...] = jnp.zeros_like(rid)
    cid[...] = jnp.zeros_like(cid)
    genes = gc_ref.shape[0]
    share = pl.cdiv(genes, people - 2)

    def first_half(step, end):
        ring_step(0, step)
        begin = (step - 1) * share
        return lax.fori_loop(jnp.minimum(begin, genes), jnp.minimum(begin + share, genes), gene_step, end)

    lax.fori_loop(1, people - 1, first_half, jnp.int32(0))
    ring_start(1)
    g_t[...] = g_ref[...].T
    for load in loads:
        load.wait()
    diag_terms(0)
    ring_last(0)

    busy = 4
    some = slots // busy

    def second_half(step, carry):
        ring_step(1, step)
        pair_terms(0, (step - 1) * some, step * some)
        return carry

    lax.fori_loop(1, busy + 1, second_half, 0)
    kin_out(0)

    def second_rest(step, carry):
        ring_step(1, step)
        return carry

    lax.fori_loop(busy + 1, people - 1, second_rest, 0)
    var_forward(gvar, 0)
    diag_terms(1)
    ring_last(1)
    var_forward(krvs[0], 1)
    pair_terms(1, 0, slots)
    kin_out(1)

    def ring_drain(step, carry):
        for h in range(2):
            for sub in range(SUB):
                for way in range(2):
                    ring_copy(h, step, way, sub).wait_send()
        return carry

    lax.fori_loop(0, people - 1, ring_drain, 0)
    var_finish(gvar, 0)
    var_finish(krvs[0], 1)
    var_forward(krvs[1], 2)
    var_finish(krvs[1], 2)

    width = pbuf.shape[2]
    chunk = rows // people
    tile = BLOCK
    per_tile = tile // chunk

    def sum_copy(target):
        return pltpu.make_async_remote_copy(
            src_ref=pbuf.at[target], dst_ref=rbuf.at[me],
            send_sem=sum_send.at[target], recv_sem=sum_recv.at[me],
            device_id=(target, q), device_id_type=MESH)

    for t in range(cols // tile):
        span = pl.ds(t * tile, tile)
        row_gene = rid[span, 0:1]
        for j in range(var // 2):
            for h in range(2):
                total = jnp.zeros((tile, wide), jnp.float32)
                for k in (j, j + var // 2):
                    value = jnp.dot(g_t[span, :], krvs[h][k], preferred_element_type=jnp.float32)
                    value += jnp.dot(
                        kr_t[span, :], gvar[k, :, h * wide:(h + 1) * wide], preferred_element_type=jnp.float32)
                    same = row_gene == cid[0:1, k * cols + h * wide:k * cols + (h + 1) * wide]
                    total = jnp.where(same, value, total)
                at = j * cols + h * wide
                pbuf[t * per_tile:(t + 1) * per_tile, :, at:at + wide] = (
                    total.astype(jnp.bfloat16).reshape(per_tile, chunk, wide))
        for k in range(per_tile):
            target = t * per_tile + k

            @pl.when(target != me)
            def _():
                sum_copy(target).start()

    own = rid[pl.ds(me * chunk, chunk), 0:1]
    final = pbuf[me].astype(jnp.float32)
    for step in range(1, people):
        source = lax.rem(me + step, people)
        pltpu.make_async_remote_copy(
            src_ref=pbuf.at[source], dst_ref=rbuf.at[source],
            send_sem=sum_send.at[source], recv_sem=sum_recv.at[source],
            device_id=(source, q), device_id_type=MESH).wait_recv()
        final += rbuf[source].astype(jnp.float32)
    final = final * (0.5 / math.sqrt(rows * people))
    for k in range(2):
        same = own == cid[0:1, k * width:(k + 1) * width]
        out_ref[:, k * width:(k + 1) * width] = jnp.where(same, final, 0.0)
    for step in range(1, people):
        sum_copy(lax.rem(me + step, people)).wait_send()


def body(people, var, genotypes, kin_diag, kin_blocks, kin_pairs, pair_count, gene_counts):
    rows, cols = genotypes.shape
    total = cols * var
    chunk = rows // people
    ny = var // CORES
    bf16, f32 = jnp.bfloat16, jnp.float32
    anywhere = pl.BlockSpec(memory_space=pl.ANY)
    vmem = pl.BlockSpec(memory_space=pltpu.VMEM)
    smem = pl.BlockSpec(memory_space=pltpu.SMEM)
    dma = pltpu.SemaphoreType.DMA
    return pl.pallas_call(
        functools.partial(kernel, people, var),
        out_shape=jax.ShapeDtypeStruct((chunk, total), f32),
        in_specs=[vmem, anywhere, anywhere, smem, smem, smem],
        out_specs=vmem,
        scratch_shapes=[
            pltpu.VMEM((2 * people, BLOCK, cols // 2), bf16),
            pltpu.VMEM((2 * people, BLOCK, cols // 2), bf16),
            pltpu.VMEM((var, rows, cols), bf16),
            pltpu.VMEM((var, rows, cols // 2), bf16),
            pltpu.VMEM((var, rows, cols // 2), bf16),
            pltpu.VMEM(kin_diag.shape, bf16),
            pltpu.VMEM(kin_blocks.shape, bf16),
            pltpu.VMEM((2, BLOCK, cols // 2), f32),
            pltpu.VMEM((cols, rows), bf16),
            pltpu.VMEM((cols, rows), bf16),
            pltpu.VMEM((people, chunk, total // 2), bf16),
            pltpu.VMEM((people, chunk, total // 2), bf16),
            pltpu.VMEM((cols, 128), jnp.int32),
            pltpu.VMEM((8, total), jnp.int32),
            dma((2, people - 1, 2, SUB)),
            dma((2, people - 1, 2, SUB)),
            dma((3, 2 * ny - 1)),
            dma((3, 2 * ny - 1)),
            dma((people,)),
            dma((people,)),
            dma((2,)),
        ],
        compiler_params=pltpu.CompilerParams(
            collective_id=0, has_side_effects=True, vmem_limit_bytes=56 << 20),
    )(genotypes, kin_diag, kin_blocks, kin_pairs.T, pair_count, gene_counts)


def solution(mesh):
    placed = (P("people", "var"), P("people", None, None), P("people", None, None), P(), P(), P())
    return jax.shard_map(
        functools.partial(body, mesh.shape["people"], mesh.shape["var"]),
        mesh=mesh, in_specs=placed, out_specs=P(("var", "people"), None), check_vma=False,
    )
```

```python
import functools
import math

import jax
import jax.numpy as jnp
from jax import lax
from jax.experimental import pallas as pl
from jax.experimental.pallas import tpu as pltpu
from jax.sharding import PartitionSpec as P

BLOCK = 256
SUB = 4
CORES = 2
MESH = pl.DeviceIdType.MESH


def ring_place(index, nz, nx):
    z, x = index // nx, index % nx
    back = nz - 1 - z
    along = jnp.where(back % 2 == 0, x - 1, nx - 1 - x)
    return jnp.where(x == 0, z, nz + back * (nx - 1) + along)


def ring_index(place, nz, nx):
    rest = jnp.where(place < nz, 0, place - nz)
    back, along = rest // (nx - 1), rest % (nx - 1)
    x = jnp.where(back % 2 == 0, 1 + along, nx - 1 - along)
    return jnp.where(place < nz, place * nx, (nz - 1 - back) * nx + x)


def kernel(people, var, g_ref, kd_hbm, kb_hbm, pairs_ref, cnt_ref, gc_ref, out_ref,
           gall_a, gall_b, gvar, krv_a, krv_b, kd, kb, acc, g_t, kr_t, pbuf, rbuf, rid, cid,
           ring_send, ring_recv, var_send, var_recv, sum_send, sum_recv, load_sem):
    rows, cols = g_ref.shape
    wide = cols // 2
    nx = math.isqrt(people // 2)
    nz = people // nx
    ny = var // CORES
    slots = kb.shape[0]
    galls, krvs = (gall_a, gall_b), (krv_a, krv_b)
    me, q = lax.axis_index("people"), lax.axis_index("var")
    y, core = q // CORES, q % CORES
    other = y * CORES + (CORES - 1 - core)

    loads = [
        pltpu.make_async_copy(kd_hbm, kd, load_sem.at[0]),
        pltpu.make_async_copy(kb_hbm, kb, load_sem.at[1]),
    ]
    for load in loads:
        load.start()

    barrier = pltpu.get_barrier_semaphore()
    for step in range(1, people):
        pl.semaphore_signal(barrier, inc=1, device_id=(lax.rem(me + step, people), q), device_id_type=MESH)
    for step in range(1, var):
        pl.semaphore_signal(barrier, inc=1, device_id=(me, lax.rem(q + step, var)), device_id_type=MESH)

    for h in range(2):
        for half in range(2):
            galls[h][2 * me + half] = g_ref[pl.ds(half * BLOCK, BLOCK), h * wide:(h + 1) * wide]
    gvar[q] = g_ref[...]
    pl.semaphore_wait(barrier, people + var - 2)

    place = ring_place(me, nz, nx)
    right = ring_index(lax.rem(place + 1, people), nz, nx)
    left = ring_index(lax.rem(place + people - 1, people), nz, nx)
    part = BLOCK // SUB

    def ring_copy(h, step, way, sub):
        shift = people - step if way == 0 else step
        source = ring_index(lax.rem(place + shift, people), nz, nx)
        view = galls[h].at[2 * source + way, pl.ds(sub * part, part)]
        return pltpu.make_async_remote_copy(
            src_ref=view, dst_ref=view,
            send_sem=ring_send.at[h, step, way, sub], recv_sem=ring_recv.at[h, step, way, sub],
            device_id=(right if way == 0 else left, q), device_id_type=MESH)

    def ring_start(h):
        for sub in range(SUB):
            for way in range(2):
                ring_copy(h, 0, way, sub).start()

    def ring_step(h, step, work, carry):
        for sub in range(SUB):
            for way in range(2):
                ring_copy(h, step - 1, way, sub).wait_recv()
                ring_copy(h, step, way, sub).start()
                carry = work(((step - 1) * SUB + sub) * 2 + way, carry)
        return carry

    def ring_last(h):
        for sub in range(SUB):
            for way in range(2):
                ring_copy(h, people - 2, way, sub).wait_recv()

    def var_copy(buf, use, slot, target, sem):
        return pltpu.make_async_remote_copy(
            src_ref=buf.at[slot], dst_ref=buf.at[slot],
            send_sem=var_send.at[use, sem], recv_sem=var_recv.at[use, sem],
            device_id=(me, target), device_id_type=MESH)

    def var_first(buf, use):
        for dy in range(1, ny):
            var_copy(buf, use, q, lax.rem(y + dy, ny) * CORES + core, dy - 1).start()
        var_copy(buf, use, q, other, ny - 1).start()

    def var_forward(buf, use):
        for dy in range(1, ny):
            slot = lax.rem(y + ny - dy, ny) * CORES + core
            var_copy(buf, use, slot, other, dy - 1).wait_recv()
            var_copy(buf, use, slot, other, ny - 1 + dy).start()

    def var_finish(buf, use):
        for sem in range(ny - 1, 2 * ny - 1):
            var_copy(buf, use, q, other, sem).wait_recv()
        for sem in range(2 * ny - 1):
            var_copy(buf, use, q, other, sem).wait_send()

    def gene_step(gene, end):
        end = end + gc_ref[gene]
        row_ids = q * cols + lax.broadcasted_iota(jnp.int32, rid.shape, 0)
        col_ids = lax.broadcasted_iota(jnp.int32, cid.shape, 1)
        rid[...] += (row_ids >= end).astype(jnp.int32)
        cid[...] += (col_ids >= end).astype(jnp.int32)
        return end

    def diag_terms(h):
        for half in range(2):
            acc[half] = jnp.dot(
                kd[half], g_ref[pl.ds(half * BLOCK, BLOCK), h * wide:(h + 1) * wide],
                preferred_element_type=jnp.float32)

    def pair_terms(h, first, count):
        picks, lefts = [], ([], [])
        for slot in (first + k for k in range(count)):
            row = pairs_ref[0, me * slots + slot] - me * 2
            live = slot < cnt_ref[me]
            picks.append(galls[h][pairs_ref[1, me * slots + slot]])
            for half in range(2):
                weight = jnp.where(live & (row == half), 1.0, 0.0).astype(jnp.bfloat16)
                lefts[half].append(kb[slot] * weight)
        picks = jnp.concatenate(picks, axis=0)
        for half in range(2):
            acc[half] += jnp.dot(
                jnp.concatenate(lefts[half], axis=1), picks, preferred_element_type=jnp.float32)

    def kin_out(h):
        for half in range(2):
            krvs[h][q, pl.ds(half * BLOCK, BLOCK), :] = acc[half].astype(jnp.bfloat16)
        var_first(krvs[h], 1 + h)
        kr_t[h * wide:(h + 1) * wide, :] = krvs[h][q].T

    ring_start(0)
    var_first(gvar, 0)
    rid[...] = jnp.zeros_like(rid)
    cid[...] = jnp.zeros_like(cid)
    genes = gc_ref.shape[0]
    share = pl.cdiv(genes, (people - 2) * 2 * SUB)

    def some_genes(turn, end):
        begin = turn * share
        return lax.fori_loop(jnp.minimum(begin, genes), jnp.minimum(begin + share, genes), gene_step, end)

    lax.fori_loop(1, people - 1, lambda step, end: ring_step(0, step, some_genes, end), jnp.int32(0))
    ring_start(1)
    g_t[...] = g_ref[...].T
    for load in loads:
        load.wait()
    diag_terms(0)
    ring_last(0)

    busy = 4
    some = slots // (busy * 2 * SUB)

    def some_pairs(turn, carry):
        pair_terms(0, turn * some, some)
        return carry

    def no_work(turn, carry):
        return carry

    lax.fori_loop(1, busy + 1, lambda step, carry: ring_step(1, step, some_pairs, carry), 0)
    kin_out(0)

    lax.fori_loop(busy + 1, people - 1, lambda step, carry: ring_step(1, step, no_work, carry), 0)
    var_forward(gvar, 0)
    diag_terms(1)
    ring_last(1)
    var_forward(krvs[0], 1)

    def group_step(group, carry):
        pair_terms(1, group * 4, 4)
        return carry

    lax.fori_loop(0, slots // 4, group_step, 0)
    kin_out(1)
    var_finish(gvar, 0)
    var_finish(krvs[0], 1)

    chunk = rows // people
    tile = BLOCK
    per_tile = tile // chunk

    def sum_copy(h, target):
        return pltpu.make_async_remote_copy(
            src_ref=pbuf.at[h, target], dst_ref=rbuf.at[h, me],
            send_sem=sum_send.at[h, target], recv_sem=sum_recv.at[h, me],
            device_id=(target, q), device_id_type=MESH)

    def sums(h):
        for t in range(cols // tile):
            span = pl.ds(t * tile, tile)
            row_gene = rid[span, 0:1]
            for j in range(var // 2):
                total = jnp.zeros((tile, wide), jnp.float32)
                for k in (j, j + var // 2):
                    value = jnp.dot(g_t[span, :], krvs[h][k], preferred_element_type=jnp.float32)
                    value += jnp.dot(
                        kr_t[span, :], gvar[k, :, h * wide:(h + 1) * wide], preferred_element_type=jnp.float32)
                    same = row_gene == cid[0:1, k * cols + h * wide:k * cols + (h + 1) * wide]
                    total = jnp.where(same, value, total)
                pbuf[h, t * per_tile:(t + 1) * per_tile, :, j * wide:(j + 1) * wide] = (
                    total.astype(jnp.bfloat16).reshape(per_tile, chunk, wide))
            for k in range(per_tile):
                target = t * per_tile + k

                @pl.when(target != me)
                def _():
                    sum_copy(h, target).start()

    sums(0)
    var_forward(krvs[1], 2)

    def ring_drain(step, carry):
        for h in range(2):
            for sub in range(SUB):
                for way in range(2):
                    ring_copy(h, step, way, sub).wait_send()
        return carry

    lax.fori_loop(0, people - 1, ring_drain, 0)
    var_finish(krvs[1], 2)
    sums(1)

    own = rid[pl.ds(me * chunk, chunk), 0:1]
    for h in range(2):
        final = pbuf[h, me].astype(jnp.float32)
        for step in range(1, people):
            source = lax.rem(me + step, people)
            pltpu.make_async_remote_copy(
                src_ref=pbuf.at[h, source], dst_ref=rbuf.at[h, source],
                send_sem=sum_send.at[h, source], recv_sem=sum_recv.at[h, source],
                device_id=(source, q), device_id_type=MESH).wait_recv()
            final += rbuf[h, source].astype(jnp.float32)
        final = final * (0.5 / math.sqrt(rows * people))
        for k in range(var):
            at, j = k * cols + h * wide, k % (var // 2)
            same = own == cid[0:1, at:at + wide]
            out_ref[:, at:at + wide] = jnp.where(same, final[:, j * wide:(j + 1) * wide], 0.0)
    for h in range(2):
        for step in range(1, people):
            sum_copy(h, lax.rem(me + step, people)).wait_send()


def body(people, var, genotypes, kin_diag, kin_blocks, kin_pairs, pair_count, gene_counts):
    rows, cols = genotypes.shape
    total = cols * var
    chunk = rows // people
    ny = var // CORES
    bf16, f32 = jnp.bfloat16, jnp.float32
    anywhere = pl.BlockSpec(memory_space=pl.ANY)
    vmem = pl.BlockSpec(memory_space=pltpu.VMEM)
    smem = pl.BlockSpec(memory_space=pltpu.SMEM)
    dma = pltpu.SemaphoreType.DMA
    return pl.pallas_call(
        functools.partial(kernel, people, var),
        out_shape=jax.ShapeDtypeStruct((chunk, total), f32),
        in_specs=[vmem, anywhere, anywhere, smem, smem, smem],
        out_specs=vmem,
        scratch_shapes=[
            pltpu.VMEM((2 * people, BLOCK, cols // 2), bf16),
            pltpu.VMEM((2 * people, BLOCK, cols // 2), bf16),
            pltpu.VMEM((var, rows, cols), bf16),
            pltpu.VMEM((var, rows, cols // 2), bf16),
            pltpu.VMEM((var, rows, cols // 2), bf16),
            pltpu.VMEM(kin_diag.shape, bf16),
            pltpu.VMEM(kin_blocks.shape, bf16),
            pltpu.VMEM((2, BLOCK, cols // 2), f32),
            pltpu.VMEM((cols, rows), bf16),
            pltpu.VMEM((cols, rows), bf16),
            pltpu.VMEM((2, people, chunk, total // 4), bf16),
            pltpu.VMEM((2, people, chunk, total // 4), bf16),
            pltpu.VMEM((cols, 128), jnp.int32),
            pltpu.VMEM((8, total), jnp.int32),
            dma((2, people - 1, 2, SUB)),
            dma((2, people - 1, 2, SUB)),
            dma((3, 2 * ny - 1)),
            dma((3, 2 * ny - 1)),
            dma((2, people)),
            dma((2, people)),
            dma((2,)),
        ],
        compiler_params=pltpu.CompilerParams(
            collective_id=0, has_side_effects=True, vmem_limit_bytes=56 << 20),
    )(genotypes, kin_diag, kin_blocks, kin_pairs.T, pair_count, gene_counts)


def solution(mesh):
    placed = (P("people", "var"), P("people", None, None), P("people", None, None), P(), P(), P())
    return jax.shard_map(
        functools.partial(body, mesh.shape["people"], mesh.shape["var"]),
        mesh=mesh, in_specs=placed, out_specs=P(("var", "people"), None), check_vma=False,
    )
```

```python
import functools
import math

import jax
import jax.numpy as jnp
from jax import lax
from jax.experimental import pallas as pl
from jax.experimental.pallas import tpu as pltpu
from jax.sharding import PartitionSpec as P

BLOCK = 256
SUB = 8
CORES = 2
MESH = pl.DeviceIdType.MESH


def ring_place(index, nz, nx):
    z, x = index // nx, index % nx
    back = nz - 1 - z
    along = jnp.where(back % 2 == 0, x - 1, nx - 1 - x)
    return jnp.where(x == 0, z, nz + back * (nx - 1) + along)


def ring_index(place, nz, nx):
    rest = jnp.where(place < nz, 0, place - nz)
    back, along = rest // (nx - 1), rest % (nx - 1)
    x = jnp.where(back % 2 == 0, 1 + along, nx - 1 - along)
    return jnp.where(place < nz, place * nx, (nz - 1 - back) * nx + x)


def kernel(people, var, g_ref, kd_hbm, kb_hbm, pairs_ref, cnt_ref, gc_ref, out_ref,
           gall_a, gall_b, gvar, krv_a, krv_b, kd, kb, acc, g_t, kr_t, pbuf, rbuf, rid, cid,
           ring_send, ring_recv, var_send, var_recv, sum_send, sum_recv, load_sem):
    rows, cols = g_ref.shape
    wide = cols // 2
    nx = math.isqrt(people // 2)
    nz = people // nx
    ny = var // CORES
    slots = kb.shape[0]
    galls, krvs = (gall_a, gall_b), (krv_a, krv_b)
    me, q = lax.axis_index("people"), lax.axis_index("var")
    y, core = q // CORES, q % CORES
    other = y * CORES + (CORES - 1 - core)

    loads = [
        pltpu.make_async_copy(kd_hbm, kd, load_sem.at[0]),
        pltpu.make_async_copy(kb_hbm, kb, load_sem.at[1]),
    ]
    for load in loads:
        load.start()

    barrier = pltpu.get_barrier_semaphore()
    for step in range(1, people):
        pl.semaphore_signal(barrier, inc=1, device_id=(lax.rem(me + step, people), q), device_id_type=MESH)
    for step in range(1, var):
        pl.semaphore_signal(barrier, inc=1, device_id=(me, lax.rem(q + step, var)), device_id_type=MESH)

    for h in range(2):
        for half in range(2):
            galls[h][2 * me + half] = g_ref[pl.ds(half * BLOCK, BLOCK), h * wide:(h + 1) * wide]
    gvar[q] = g_ref[...]
    pl.semaphore_wait(barrier, people + var - 2)

    place = ring_place(me, nz, nx)
    right = ring_index(lax.rem(place + 1, people), nz, nx)
    left = ring_index(lax.rem(place + people - 1, people), nz, nx)
    part = BLOCK // SUB

    def ring_copy(h, step, way, sub):
        shift = people - step if way == 0 else step
        source = ring_index(lax.rem(place + shift, people), nz, nx)
        view = galls[h].at[2 * source + way, pl.ds(sub * part, part)]
        return pltpu.make_async_remote_copy(
            src_ref=view, dst_ref=view,
            send_sem=ring_send.at[h, step, way, sub], recv_sem=ring_recv.at[h, step, way, sub],
            device_id=(right if way == 0 else left, q), device_id_type=MESH)

    def ring_start(h):
        for sub in range(SUB):
            for way in range(2):
                ring_copy(h, 0, way, sub).start()

    def ring_step(h, step, work, carry):
        for sub in range(SUB):
            for way in range(2):
                ring_copy(h, step - 1, way, sub).wait_recv()
                ring_copy(h, step, way, sub).start()
                carry = work(((step - 1) * SUB + sub) * 2 + way, carry)
        return carry

    def ring_last(h):
        for sub in range(SUB):
            for way in range(2):
                ring_copy(h, people - 2, way, sub).wait_recv()

    def var_copy(buf, use, slot, target, sem):
        return pltpu.make_async_remote_copy(
            src_ref=buf.at[slot], dst_ref=buf.at[slot],
            send_sem=var_send.at[use, sem], recv_sem=var_recv.at[use, sem],
            device_id=(me, target), device_id_type=MESH)

    def var_first(buf, use):
        for dy in range(1, ny):
            var_copy(buf, use, q, lax.rem(y + dy, ny) * CORES + core, dy - 1).start()
        var_copy(buf, use, q, other, ny - 1).start()

    def var_forward(buf, use):
        for dy in range(1, ny):
            slot = lax.rem(y + ny - dy, ny) * CORES + core
            var_copy(buf, use, slot, other, dy - 1).wait_recv()
            var_copy(buf, use, slot, other, ny - 1 + dy).start()

    def var_finish(buf, use):
        for sem in range(ny - 1, 2 * ny - 1):
            var_copy(buf, use, q, other, sem).wait_recv()
        for sem in range(2 * ny - 1):
            var_copy(buf, use, q, other, sem).wait_send()

    def gene_step(gene, end):
        end = end + gc_ref[gene]
        row_ids = q * cols + lax.broadcasted_iota(jnp.int32, rid.shape, 0)
        col_ids = lax.broadcasted_iota(jnp.int32, cid.shape, 1)
        rid[...] += (row_ids >= end).astype(jnp.int32)
        cid[...] += (col_ids >= end).astype(jnp.int32)
        return end

    def diag_terms(h):
        for half in range(2):
            acc[half] = jnp.dot(
                kd[half], g_ref[pl.ds(half * BLOCK, BLOCK), h * wide:(h + 1) * wide],
                preferred_element_type=jnp.float32)

    def pair_terms(h, first, count):
        picks, lefts = [], ([], [])
        for slot in (first + k for k in range(count)):
            row = pairs_ref[0, me * slots + slot] - me * 2
            live = slot < cnt_ref[me]
            picks.append(galls[h][pairs_ref[1, me * slots + slot]])
            for half in range(2):
                weight = jnp.where(live & (row == half), 1.0, 0.0).astype(jnp.bfloat16)
                lefts[half].append(kb[slot] * weight)
        picks = jnp.concatenate(picks, axis=0)
        for half in range(2):
            acc[half] += jnp.dot(
                jnp.concatenate(lefts[half], axis=1), picks, preferred_element_type=jnp.float32)

    def kin_out(h):
        for half in range(2):
            krvs[h][q, pl.ds(half * BLOCK, BLOCK), :] = acc[half].astype(jnp.bfloat16)
        var_first(krvs[h], 1 + h)
        kr_t[h * wide:(h + 1) * wide, :] = krvs[h][q].T

    ring_start(0)
    var_first(gvar, 0)
    rid[...] = jnp.zeros_like(rid)
    cid[...] = jnp.zeros_like(cid)
    genes = gc_ref.shape[0]
    share = pl.cdiv(genes, (people - 2) * 2 * SUB)

    def some_genes(turn, end):
        begin = turn * share
        return lax.fori_loop(jnp.minimum(begin, genes), jnp.minimum(begin + share, genes), gene_step, end)

    lax.fori_loop(1, people - 1, lambda step, end: ring_step(0, step, some_genes, end), jnp.int32(0))
    ring_start(1)
    g_t[...] = g_ref[...].T
    for load in loads:
        load.wait()
    diag_terms(0)
    ring_last(0)

    busy = 2
    some = slots // (busy * 2 * SUB)

    def some_pairs(turn, carry):
        pair_terms(0, turn * some, some)
        return carry

    def no_work(turn, carry):
        return carry

    lax.fori_loop(1, busy + 1, lambda step, carry: ring_step(1, step, some_pairs, carry), 0)
    kin_out(0)

    lax.fori_loop(busy + 1, people - 1, lambda step, carry: ring_step(1, step, no_work, carry), 0)
    var_forward(gvar, 0)
    diag_terms(1)
    ring_last(1)
    var_forward(krvs[0], 1)

    def group_step(group, carry):
        pair_terms(1, group * 4, 4)
        return carry

    lax.fori_loop(0, slots // 4, group_step, 0)
    kin_out(1)
    var_finish(gvar, 0)
    var_finish(krvs[0], 1)

    chunk = rows // people
    tile = BLOCK
    per_tile = tile // chunk

    def sum_copy(h, target):
        return pltpu.make_async_remote_copy(
            src_ref=pbuf.at[h, target], dst_ref=rbuf.at[h, me],
            send_sem=sum_send.at[h, target], recv_sem=sum_recv.at[h, me],
            device_id=(target, q), device_id_type=MESH)

    def sums(h):
        for t in range(cols // tile):
            span = pl.ds(t * tile, tile)
            row_gene = rid[span, 0:1]
            for j in range(var // 2):
                total = jnp.zeros((tile, wide), jnp.float32)
                for k in (j, j + var // 2):
                    value = jnp.dot(g_t[span, :], krvs[h][k], preferred_element_type=jnp.float32)
                    value += jnp.dot(
                        kr_t[span, :], gvar[k, :, h * wide:(h + 1) * wide], preferred_element_type=jnp.float32)
                    same = row_gene == cid[0:1, k * cols + h * wide:k * cols + (h + 1) * wide]
                    total = jnp.where(same, value, total)
                pbuf[h, t * per_tile:(t + 1) * per_tile, :, j * wide:(j + 1) * wide] = (
                    total.astype(jnp.bfloat16).reshape(per_tile, chunk, wide))
            for k in range(per_tile):
                target = t * per_tile + k

                @pl.when(target != me)
                def _():
                    sum_copy(h, target).start()

    sums(0)
    var_forward(krvs[1], 2)

    def ring_drain(step, carry):
        for h in range(2):
            for sub in range(SUB):
                for way in range(2):
                    ring_copy(h, step, way, sub).wait_send()
        return carry

    lax.fori_loop(0, people - 1, ring_drain, 0)
    var_finish(krvs[1], 2)
    sums(1)

    own = rid[pl.ds(me * chunk, chunk), 0:1]
    for h in range(2):
        final = pbuf[h, me].astype(jnp.float32)
        for step in range(1, people):
            source = lax.rem(me + step, people)
            pltpu.make_async_remote_copy(
                src_ref=pbuf.at[h, source], dst_ref=rbuf.at[h, source],
                send_sem=sum_send.at[h, source], recv_sem=sum_recv.at[h, source],
                device_id=(source, q), device_id_type=MESH).wait_recv()
            final += rbuf[h, source].astype(jnp.float32)
        final = final * (0.5 / math.sqrt(rows * people))
        for k in range(var):
            at, j = k * cols + h * wide, k % (var // 2)
            same = own == cid[0:1, at:at + wide]
            out_ref[:, at:at + wide] = jnp.where(same, final[:, j * wide:(j + 1) * wide], 0.0)
    for h in range(2):
        for step in range(1, people):
            sum_copy(h, lax.rem(me + step, people)).wait_send()


def body(people, var, genotypes, kin_diag, kin_blocks, kin_pairs, pair_count, gene_counts):
    rows, cols = genotypes.shape
    total = cols * var
    chunk = rows // people
    ny = var // CORES
    bf16, f32 = jnp.bfloat16, jnp.float32
    anywhere = pl.BlockSpec(memory_space=pl.ANY)
    vmem = pl.BlockSpec(memory_space=pltpu.VMEM)
    smem = pl.BlockSpec(memory_space=pltpu.SMEM)
    dma = pltpu.SemaphoreType.DMA
    return pl.pallas_call(
        functools.partial(kernel, people, var),
        out_shape=jax.ShapeDtypeStruct((chunk, total), f32),
        in_specs=[vmem, anywhere, anywhere, smem, smem, smem],
        out_specs=vmem,
        scratch_shapes=[
            pltpu.VMEM((2 * people, BLOCK, cols // 2), bf16),
            pltpu.VMEM((2 * people, BLOCK, cols // 2), bf16),
            pltpu.VMEM((var, rows, cols), bf16),
            pltpu.VMEM((var, rows, cols // 2), bf16),
            pltpu.VMEM((var, rows, cols // 2), bf16),
            pltpu.VMEM(kin_diag.shape, bf16),
            pltpu.VMEM(kin_blocks.shape, bf16),
            pltpu.VMEM((2, BLOCK, cols // 2), f32),
            pltpu.VMEM((cols, rows), bf16),
            pltpu.VMEM((cols, rows), bf16),
            pltpu.VMEM((2, people, chunk, total // 4), bf16),
            pltpu.VMEM((2, people, chunk, total // 4), bf16),
            pltpu.VMEM((cols, 128), jnp.int32),
            pltpu.VMEM((8, total), jnp.int32),
            dma((2, people - 1, 2, SUB)),
            dma((2, people - 1, 2, SUB)),
            dma((3, 2 * ny - 1)),
            dma((3, 2 * ny - 1)),
            dma((2, people)),
            dma((2, people)),
            dma((2,)),
        ],
        compiler_params=pltpu.CompilerParams(
            collective_id=0, has_side_effects=True, vmem_limit_bytes=56 << 20),
    )(genotypes, kin_diag, kin_blocks, kin_pairs.T, pair_count, gene_counts)


def solution(mesh):
    placed = (P("people", "var"), P("people", None, None), P("people", None, None), P(), P(), P())
    return jax.shard_map(
        functools.partial(body, mesh.shape["people"], mesh.shape["var"]),
        mesh=mesh, in_specs=placed, out_specs=P(("var", "people"), None), check_vma=False,
    )
```
